128 devices in a mesh: fsdp: 8 (over z, x_hi), ctx: 8 (over y, core), tp: 2 (over x_lo).
Axes of the slice: x: 4 (x_hi: 2, x_lo: 2; x = x_hi * 2 + x_lo), y: 4, z: 4, core: 2. Of those that a mesh axis runs over, the one named last changes fastest.
Arguments:
- inputs: float32 [8, 1024, 1152], P('fsdp', 'ctx'), may hold values from -6 to 6
- positions: int32 [8, 1024], P('fsdp', 'ctx'), may hold values from 0 to 959, as said below
- norm_gains: bfloat16 [1152, 4], P('fsdp'), may hold values from 0.5 to 1.5
- head_gains: bfloat16 [2, 256], replicated, may hold values from 0.3984375 to 1.59375
- attn_split: bfloat16 [1152, 2, 1024], P('fsdp', None, 'tp'), may hold values from -0.1875 to 0.1875
- attn_shared: bfloat16 [1152, 2, 256], P('fsdp'), may hold values from -0.1875 to 0.1875
- ffn_gate_up: bfloat16 [1152, 2, 6912], P('fsdp', None, 'tp'), may hold values from -0.1875 to 0.1875
- ffn_down: bfloat16 [1152, 6912], P('fsdp', 'tp'), may hold values from -0.078125 to 0.078125
- cotangent: float32 [8, 1024, 1152], P('fsdp', 'ctx'), may hold values from -6 to 6
Outputs:
- output: float32 [8, 1024, 1152], P('fsdp', 'ctx')
- d_inputs: float32 [8, 1024, 1152], P('fsdp', 'ctx')
- d_norm_gains: float32 [1152, 4], P('fsdp')
- d_head_gains: float32 [2, 256], replicated
- d_attn_split: float32 [1152, 2, 1024], P('fsdp', None, 'tp')
- d_attn_shared: float32 [1152, 2, 256], P('fsdp')
- d_gate_up: float32 [1152, 2, 6912], P('fsdp', None, 'tp')
- d_down: float32 [1152, 6912], P('fsdp', 'tp')
The draws below stay inside these ranges and needn't reach their ends.
Inputs may be any that keep to these rules, and one draw needn't show every extreme that they name: `positions`: each sequence is packed with documents of 64 to 960 tokens, the last one possibly cut by the sequence's end; a token's position counts from its document's first token.
All inputs are finite; a program needn't handle non-finite values.
Results may differ from the reference program's by a relative error of at most 0.025.
Values may be sent and summed in bfloat16 or wider, within the bound.
No kernel may reach another device: no remote copies, remote signals or barrier semaphores. Data moves between devices by JAX's collectives and lax.ppermute only.
A program may use at most 192 MiB of HBM per device.

```python
import jax
import jax.numpy as jnp
from jax import lax

D = 1152
HEADS = 4
HD = 256
FF = 6912
LENGTH = 1024
SEQS = 8
MOSTLEN = 960
LEAST = 64


def draw_positions(key, part):
    doc_count = LENGTH // LEAST + 2
    doc_lengths = jax.random.randint(key, (SEQS, doc_count), LEAST, MOSTLEN + 1)
    doc_lengths = doc_lengths.at[0, 0].set(MOSTLEN)
    starts = jnp.cumsum(doc_lengths, axis=1) - doc_lengths
    index = jnp.arange(LENGTH, dtype=jnp.int32)
    within = starts[:, None, :] <= index[None, :, None]
    begin = jnp.max(jnp.where(within, starts[:, None, :], 0), axis=2)
    return (index[None, :] - begin).astype(jnp.int32)


def levels(rng, extent, pieces, smallest, top_value):
    def one(dim, shards_of):
        draws = jax.random.uniform(jax.random.fold_in(jax.random.fold_in(rng, 6), dim), (shards_of,), jnp.float32, smallest / len(pieces), top_value / len(pieces))
        return jnp.repeat(jnp.exp(draws), extent[dim] // shards_of).reshape((-1,) + (1,) * (len(extent) - dim - 1))

    loudness = one(*pieces[0])
    for cut in pieces[1:]:
        loudness = loudness * one(*cut)
    return loudness


def gaussian(stream_key, extent, spread, bound, cuts=(), held_as=jnp.bfloat16):
    values = jax.random.normal(stream_key, extent, jnp.float32) * spread
    if len(cuts) > 0:
        values = levels(stream_key, extent, cuts, -0.22, 0.18) * values
    return jnp.clip(values, min=-bound, max=bound).astype(held_as)


def setup_inputs(seed: int = 0) -> dict:
    splits = jax.random.split(jax.random.key(seed), 10)
    return {
        "inputs": gaussian(splits[0], (SEQS, LENGTH, D), 1.0, 6.0, ((0, 8), (1, 8)), jnp.float32),
        "positions": draw_positions(jax.random.fold_in(splits[9], 71), 0),
        "norm_gains": jnp.clip(1.0 + 0.1 * jax.random.normal(splits[2], (D, 4), jnp.float32), 0.5, 1.5).astype(jnp.bfloat16),
        "head_gains": jnp.clip(1.0 + 0.12 * jax.random.normal(splits[3], (2, HD), jnp.float32), 0.3984375, 1.59375).astype(jnp.bfloat16),
        "attn_split": gaussian(splits[4], (D, 2, HEADS * HD), D ** -0.5, 0.1875, ((0, 8), (2, 2))),
        "attn_shared": gaussian(splits[5], (D, 2, HD), D ** -0.5, 0.1875, ((0, 8),)),
        "ffn_gate_up": gaussian(splits[6], (D, 2, FF), D ** -0.5, 0.1875, ((0, 8), (2, 2))),
        "ffn_down": gaussian(splits[7], (D, FF), FF ** -0.5, 0.078125, ((0, 8), (1, 2))),
        "cotangent": gaussian(splits[8], (SEQS, LENGTH, D), 1.0, 6.0, ((0, 8), (1, 8)), jnp.float32),
    }


EPSILON = 1e-06
ROPE_BASE = 1000000.0
MASKED_SCORE = -1e+30

def inv_rms(values):
    return lax.rsqrt(lax.optimization_barrier(jnp.mean(values * values, axis=-1, keepdims=True)) + EPSILON)

def rms_back(values, scale_rows, cot_scaled):
    return scale_rows * cot_scaled - values * scale_rows ** 3 * lax.optimization_barrier(jnp.mean(values * cot_scaled, axis=-1, keepdims=True))

def gelu_tanh(values):
    return 0.5 * values * (1.0 + jnp.tanh(0.7978845608028654 * (values + 0.044715 * values ** 3)))

def rotate(values, cos_table, sin_table):
    middle = values.shape[-1] // 2
    upper_half = values[..., :middle]
    lower_half = values[..., middle:]
    return jnp.concatenate([upper_half * cos_table - lower_half * sin_table, lower_half * cos_table + upper_half * sin_table], axis=-1)

def rotate_back(values, cos_table, sin_table):
    middle = values.shape[-1] // 2
    upper_half = values[..., :middle]
    lower_half = values[..., middle:]
    return jnp.concatenate([upper_half * cos_table + lower_half * sin_table, lower_half * cos_table - upper_half * sin_table], axis=-1)

def dot_last(left, right):
    return lax.dot_general(left, right, (((1,), (1,)), ((), ())), preferred_element_type=jnp.float32)

def dot_first(left, right):
    return lax.dot_general(left, right, (((0,), (0,)), ((), ())), preferred_element_type=jnp.float32)

def reference(inputs, positions, norm_gains, head_gains, attn_split, attn_shared, ffn_gate_up, ffn_down, cotangent):
    gains = norm_gains.astype(jnp.float32)
    head_scale = head_gains.astype(jnp.float32)
    w_query = attn_split[:, 0]
    w_output = attn_split[:, 1]
    w_keyval = attn_shared.reshape(D, 2 * HD)
    w_gateup = ffn_gate_up.reshape(D, 2 * FF)
    score_scale = HD ** (-0.5)
    frequency = ROPE_BASE ** (-2.0 * jnp.arange(HD // 2, dtype=jnp.float32) / HD)

    def one_sequence(carry, item):
        tokens, cot_rows, token_pos = item
        seq_len = tokens.shape[0]
        scale_in = inv_rms(tokens)
        unit_in = tokens * scale_in
        normed_in = (unit_in * gains[:, 0]).astype(jnp.bfloat16)
        queries = jnp.dot(normed_in, w_query, preferred_element_type=jnp.float32).reshape(seq_len, HEADS, HD)
        keyval = jnp.dot(normed_in, w_keyval, preferred_element_type=jnp.float32)
        key_raw = keyval[:, :HD]
        val_raw = keyval[:, HD:]
        scale_q = inv_rms(queries)
        unit_q = queries * scale_q
        scale_k = inv_rms(key_raw)
        unit_k = key_raw * scale_k
        angles = token_pos.astype(jnp.float32)[:, None] * frequency[None, :]
        cos_table = jnp.cos(angles)
        sin_table = jnp.sin(angles)
        query_bf = (rotate(unit_q * head_scale[0], cos_table[:, None], sin_table[:, None]) * score_scale).astype(jnp.bfloat16)
        key_bf = rotate(unit_k * head_scale[1], cos_table, sin_table).astype(jnp.bfloat16)
        val_bf = val_raw.astype(jnp.bfloat16)
        index = jnp.arange(seq_len, dtype=jnp.int32)
        visible = (index[None, :] <= index[:, None]) & (index[None, :] >= (index - token_pos)[:, None])
        scores = jnp.where(visible[None], jnp.einsum('chd,kd->hck', query_bf.astype(jnp.float32), key_bf.astype(jnp.float32)), MASKED_SCORE)
        row_max = lax.optimization_barrier(jnp.max(scores, axis=-1, keepdims=True))
        log_total = row_max + jnp.log(lax.optimization_barrier(jnp.sum(jnp.exp(scores - row_max), axis=-1, keepdims=True)))
        probs = jnp.exp(scores - log_total)
        probs_bf = probs.astype(jnp.bfloat16)
        attended = jnp.einsum('hck,kd->chd', probs_bf.astype(jnp.float32), val_bf.astype(jnp.float32))
        attended_bf = attended.astype(jnp.bfloat16).reshape(seq_len, HEADS * HD)
        branch_attn = dot_last(attended_bf, w_output)
        scale_attn = inv_rms(branch_attn)
        unit_attn = branch_attn * scale_attn
        hidden_in = tokens + unit_attn * gains[:, 1]
        scale_mid = inv_rms(hidden_in)
        unit_mid = hidden_in * scale_mid
        normed_mid = (unit_mid * gains[:, 2]).astype(jnp.bfloat16)
        gate_up = jnp.dot(normed_mid, w_gateup, preferred_element_type=jnp.float32).reshape(seq_len, 2, FF)
        gate_pre = gate_up[:, 0]
        up_proj = gate_up[:, 1]
        activated, gelu_grad = jax.vjp(gelu_tanh, gate_pre)
        hidden_bf = (activated * up_proj).astype(jnp.bfloat16)
        branch_ffn = dot_last(hidden_bf, ffn_down)
        scale_ffn = inv_rms(branch_ffn)
        unit_ffn = branch_ffn * scale_ffn
        result = hidden_in + unit_ffn * gains[:, 3]
        grad_ffn_bf = rms_back(branch_ffn, scale_ffn, cot_rows * gains[:, 3]).astype(jnp.bfloat16)
        grad_hidden = jnp.dot(grad_ffn_bf, ffn_down, preferred_element_type=jnp.float32)
        grad_gate = gelu_grad(grad_hidden * up_proj)[0]
        grad_up = grad_hidden * activated
        grad_gateup = jnp.stack([grad_gate, grad_up], axis=1).astype(jnp.bfloat16).reshape(seq_len, 2 * FF)
        grad_mid_in = dot_last(grad_gateup, w_gateup)
        grad_resid = cot_rows + rms_back(hidden_in, scale_mid, gains[:, 2] * grad_mid_in)
        grad_attn_bf = rms_back(branch_attn, scale_attn, gains[:, 1] * grad_resid).astype(jnp.bfloat16)
        grad_heads = jnp.dot(grad_attn_bf, w_output, preferred_element_type=jnp.float32).astype(jnp.bfloat16).reshape(seq_len, HEADS, HD)
        grad_probs = jnp.einsum('chd,kd->hck', grad_heads.astype(jnp.float32), val_bf.astype(jnp.float32))
        row_delta = lax.optimization_barrier(jnp.sum(grad_heads.astype(jnp.float32) * attended, axis=-1)).T[:, :, None]
        grad_scores_bf = (probs * (grad_probs - row_delta)).astype(jnp.bfloat16)
        grad_qrot = jnp.einsum('hck,kd->chd', grad_scores_bf.astype(jnp.float32), key_bf.astype(jnp.float32)) * score_scale
        grad_krot = jnp.einsum('hck,chd->kd', grad_scores_bf.astype(jnp.float32), query_bf.astype(jnp.float32))
        grad_vals = jnp.einsum('hck,chd->kd', probs_bf.astype(jnp.float32), grad_heads.astype(jnp.float32))
        grad_qn = rotate_back(grad_qrot, cos_table[:, None], sin_table[:, None])
        grad_q = rms_back(queries, scale_q, head_scale[0] * grad_qn)
        grad_kn = rotate_back(grad_krot, cos_table, sin_table)
        grad_k = rms_back(key_raw, scale_k, head_scale[1] * grad_kn)
        grad_q_bf = grad_q.reshape(seq_len, HEADS * HD).astype(jnp.bfloat16)
        grad_kv_bf = jnp.concatenate([grad_k, grad_vals], axis=1).astype(jnp.bfloat16)
        grad_norm_in = dot_last(grad_q_bf, w_query) + dot_last(grad_kv_bf, w_keyval)
        grad_tokens = grad_resid + rms_back(tokens, scale_in, gains[:, 0] * grad_norm_in)
        d_split, d_shared, d_gateup, d_down, d_gains, d_head = carry
        d_split = d_split + jnp.stack([dot_first(normed_in, grad_q_bf), dot_first(grad_attn_bf, attended_bf)], axis=1)
        d_shared = d_shared + dot_first(normed_in, grad_kv_bf).reshape(D, 2, HD)
        d_gateup = d_gateup + dot_first(normed_mid, grad_gateup).reshape(D, 2, FF)
        d_down = d_down + dot_first(grad_ffn_bf, hidden_bf)
        d_gains = d_gains + jnp.stack([lax.optimization_barrier(jnp.sum(unit_in * grad_norm_in, axis=0)), lax.optimization_barrier(jnp.sum(unit_attn * grad_resid, axis=0)), lax.optimization_barrier(jnp.sum(unit_mid * grad_mid_in, axis=0)), lax.optimization_barrier(jnp.sum(unit_ffn * cot_rows, axis=0))], axis=1)
        d_head = d_head + jnp.stack([lax.optimization_barrier(jnp.sum(unit_q * grad_qn, axis=(0, 1))), lax.optimization_barrier(jnp.sum(unit_k * grad_kn, axis=0))])
        return ((d_split, d_shared, d_gateup, d_down, d_gains, d_head), (result, grad_tokens))
    start = (jnp.zeros((D, 2, HEADS * HD), jnp.float32), jnp.zeros((D, 2, HD), jnp.float32), jnp.zeros((D, 2, FF), jnp.float32), jnp.zeros((D, FF), jnp.float32), jnp.zeros((D, 4), jnp.float32), jnp.zeros((2, HD), jnp.float32))
    totals, stacked = lax.scan(one_sequence, start, (inputs, cotangent, positions))
    return (stacked[0], stacked[1], totals[4], totals[5], totals[0], totals[1], totals[2], totals[3])
```

```python
import jax
import jax.numpy as jnp
from jax import lax
from jax.sharding import Mesh, PartitionSpec as P

HD = 256
EPSILON = 1e-06
ROPE_BASE = 1000000.0
MASKED_SCORE = -1e30
SIZE = {"z": 4, "xh": 2, "y": 4, "core": 2, "tp": 2}
BF = jnp.bfloat16
F32 = jnp.float32


def inv_rms(values):
    return lax.rsqrt(jnp.mean(values * values, axis=-1, keepdims=True) + EPSILON)


def rms_back(values, scale_rows, cot_scaled):
    return scale_rows * cot_scaled - values * scale_rows**3 * jnp.mean(
        values * cot_scaled, axis=-1, keepdims=True
    )


def rotate(values, cos_table, sin_table):
    middle = values.shape[-1] // 2
    upper_half = values[..., :middle]
    lower_half = values[..., middle:]
    return jnp.concatenate(
        [
            upper_half * cos_table - lower_half * sin_table,
            lower_half * cos_table + upper_half * sin_table,
        ],
        axis=-1,
    )


def rotate_back(values, cos_table, sin_table):
    return rotate(values, cos_table, -sin_table)


def dot(left, right):
    return jnp.dot(left, right, preferred_element_type=F32)


def dot_last(left, right):
    return lax.dot_general(left, right, (((1,), (1,)), ((), ())), preferred_element_type=F32)


def dot_first(left, right):
    return lax.dot_general(left, right, (((0,), (0,)), ((), ())), preferred_element_type=F32)


def send(array, axis, shift):
    n = SIZE[axis]
    return lax.ppermute(array, axis, [(i, (i + shift) % n) for i in range(n)])


def gather_rows(shard, z, xh):
    rows, cols = shard.shape
    other = send(shard, "xh", 1)
    pair = jnp.where(
        xh == 0, jnp.concatenate([shard, other], 0), jnp.concatenate([other, shard], 0)
    )
    whole = jnp.zeros((4, 2 * rows, cols), shard.dtype)
    whole = lax.dynamic_update_slice(whole, pair[None], (z, 0, 0))
    for k in range(1, 4):
        whole = lax.dynamic_update_slice(
            whole, send(pair, "z", k)[None], (lax.rem(z + 4 - k, 4), 0, 0)
        )
    return whole.reshape(8 * rows, cols)


def scatter_rows(whole, z, xh):
    total, cols = whole.shape
    rows = total // 8
    blocks = whole.astype(BF).reshape(4, 2 * rows, cols)
    pair = lax.dynamic_index_in_dim(blocks, z, 0, False).astype(F32)
    for k in range(1, 4):
        block = lax.dynamic_index_in_dim(blocks, lax.rem(z + 4 - k, 4), 0, False)
        pair = pair + send(block, "z", -k).astype(F32)
    pair = pair.astype(BF).reshape(2, rows, cols)
    away = lax.dynamic_index_in_dim(pair, 1 - xh, 0, False)
    own = lax.dynamic_index_in_dim(pair, xh, 0, False)
    return own.astype(F32) + send(away, "xh", 1).astype(F32)


def gather_tokens(block):
    mine = jnp.concatenate([block] + [send(block, "y", k) for k in range(1, 4)], 0)
    return jnp.concatenate([mine, send(mine, "core", 1)], 0)


def pair_sum(array):
    rounded = array.astype(BF)
    return rounded.astype(F32) + send(rounded, "tp", 1).astype(F32)


def scatter_tokens(partial):
    half = partial.shape[0] // 2
    local = half // 4
    away = send(partial[half:].astype(BF), "core", 1)
    mine = partial[:half] + away.astype(F32)
    rounded = mine.astype(BF)
    total = mine[:local]
    for k in range(1, 4):
        total = total + send(rounded[k * local : (k + 1) * local], "y", -k).astype(F32)
    return pair_sum(total)


def ring_sum(array):
    got = [send(array, "y", k).astype(F32) for k in range(1, 4)]
    return (array.astype(F32) + got[1]) + (got[0] + got[2])


def small_sum(array):
    array = array + send(array, "core", 1)
    array = array + send(array, "tp", 1)
    array = array + send(array, "xh", 1)
    for axis in ("y", "z"):
        got = [send(array, axis, k) for k in range(1, 4)]
        array = (array + got[1]) + (got[0] + got[2])
    return array


def swap_halves(array):
    rows, cols = array.shape
    half = 128
    parts = array.reshape(rows // (2 * half), 2, half, cols)
    return jnp.concatenate([parts[:, 1:], parts[:, :1]], 1).reshape(rows, cols)


def on_device(
    inputs,
    positions,
    norm_gains,
    head_gains,
    attn_split,
    attn_shared,
    ffn_gate_up,
    ffn_down,
    cotangent,
):
    z, xh, y, core, tp = (lax.axis_index(a) for a in ("z", "xh", "y", "core", "tp"))
    first = core == 0
    tokens = inputs[0]
    cot_rows = cotangent[0]
    local_len, model_width = tokens.shape
    shard_rows = attn_split.shape[0]
    ff_local = ffn_gate_up.shape[2] // 8
    ff_pad = 512
    place = y * 2 + core

    wq_shard = lax.dynamic_slice(attn_split, (0, 0, core * HD), (shard_rows, 1, HD))[:, 0]
    wo_shard = lax.dynamic_slice(attn_split, (0, 1, core * HD), (shard_rows, 1, HD))[:, 0]
    wkv_shard = lax.dynamic_index_in_dim(attn_shared, core, 1, False)
    gains_shard = jnp.pad(norm_gains, ((0, 0), (0, 124)))
    attn_all = gather_rows(jnp.concatenate([wq_shard, wkv_shard, gains_shard], 1), z, xh)
    gu_shard = lax.dynamic_slice(
        ffn_gate_up, (0, 0, place * ff_local), (shard_rows, 2, ff_local)
    )
    down_shard = lax.dynamic_slice(ffn_down, (0, place * ff_local), (shard_rows, ff_local))

    def padded(array):
        return jnp.pad(array, ((0, 0), (0, ff_pad - ff_local)))

    ffn_all = gather_rows(
        jnp.concatenate(
            [wo_shard, padded(gu_shard[:, 0]), padded(gu_shard[:, 1]), padded(down_shard)], 1
        ),
        z,
        xh,
    )
    w_qkv = attn_all[:, : 2 * HD]
    gains = attn_all[:, 2 * HD : 2 * HD + 4].astype(F32).T
    w_out = ffn_all[:, :HD]
    w_gateup = ffn_all[:, HD : HD + 2 * ff_pad]
    w_down = ffn_all[:, HD + 2 * ff_pad :]

    head_scale = head_gains.astype(F32)
    score_scale = HD ** (-0.5)
    frequency = ROPE_BASE ** (-2.0 * jnp.arange(HD // 2, dtype=F32) / HD)
    own_pos = positions.astype(F32)
    chip_pos = jnp.concatenate([own_pos, send(own_pos, "core", 1)], 1)[0]
    angles = chip_pos[:, None] * frequency[None, :]
    cos_table = jnp.cos(angles)
    sin_table = jnp.sin(angles)

    scale_in = inv_rms(tokens)
    unit_in = tokens * scale_in
    normed_own = (unit_in * gains[0]).astype(BF)
    normed_in = jnp.concatenate([normed_own, send(normed_own, "core", 1)], 0)
    qkv = dot(normed_in, w_qkv)
    queries = qkv[:, :HD]
    kv_raw = qkv[:, HD:]
    scale_q = inv_rms(queries)
    unit_q = queries * scale_q
    scale_k = inv_rms(kv_raw)
    unit_k = kv_raw * scale_k
    query_bf = (rotate(unit_q * head_scale[0], cos_table, sin_table) * score_scale).astype(BF)
    kv_bf = jnp.where(first, rotate(unit_k * head_scale[1], cos_table, sin_table), kv_raw).astype(
        BF
    )
    kv_mine = jnp.concatenate([kv_bf] + [send(kv_bf, "y", k) for k in range(1, 4)], 0)
    kv_other = swap_halves(send(kv_mine, "core", 1))
    keys = jnp.where(first, kv_mine, kv_other)
    vals = jnp.where(first, kv_other, kv_mine)

    chip_len = 2 * local_len
    seq_len = 4 * chip_len
    q_iota = jnp.arange(chip_len, dtype=jnp.int32)
    q_core = lax.rem(core + q_iota // local_len, 2)
    query_index = y * chip_len + q_core * local_len + lax.rem(q_iota, local_len)
    k_iota = jnp.arange(seq_len, dtype=jnp.int32)
    k_core = lax.rem(core + k_iota // local_len, 2)
    key_index = (
        lax.rem(y + 4 - k_iota // chip_len, 4) * chip_len
        + k_core * local_len
        + lax.rem(k_iota, local_len)
    )
    begin = query_index - chip_pos.astype(jnp.int32)
    visible = (key_index[None, :] <= query_index[:, None]) & (key_index[None, :] >= begin[:, None])
    scores = jnp.where(visible, dot_last(query_bf, keys), MASKED_SCORE)
    row_max = jnp.max(scores, axis=-1, keepdims=True)
    log_total = row_max + jnp.log(jnp.sum(jnp.exp(scores - row_max), axis=-1, keepdims=True))
    probs = jnp.exp(scores - log_total)
    probs_bf = probs.astype(BF)
    attended = dot(probs_bf, vals)
    attended_bf = attended.astype(BF)

    def chip_scatter(partial):
        away = send(partial[local_len:].astype(BF), "core", 1)
        return pair_sum(partial[:local_len] + away.astype(F32))

    branch_attn = chip_scatter(dot_last(attended_bf, w_out))
    scale_attn = inv_rms(branch_attn)
    unit_attn = branch_attn * scale_attn
    hidden_in = tokens + unit_attn * gains[1]
    scale_mid = inv_rms(hidden_in)
    unit_mid = hidden_in * scale_mid
    normed_mid = gather_tokens((unit_mid * gains[2]).astype(BF))

    gate_up = dot(normed_mid, w_gateup)
    gate_pre = gate_up[:, :ff_pad]
    up_proj = gate_up[:, ff_pad:]
    cube = 0.7978845608028654
    tanh_part = jnp.tanh(cube * (gate_pre + 0.044715 * gate_pre**3))
    activated = 0.5 * gate_pre * (1.0 + tanh_part)
    slope = 0.5 * (1.0 + tanh_part) + 0.5 * gate_pre * (1.0 - tanh_part * tanh_part) * cube * (
        1.0 + 3.0 * 0.044715 * gate_pre * gate_pre
    )
    hidden_bf = (activated * up_proj).astype(BF)
    branch_ffn = scatter_tokens(dot_last(hidden_bf, w_down))
    scale_ffn = inv_rms(branch_ffn)
    unit_ffn = branch_ffn * scale_ffn
    result = hidden_in + unit_ffn * gains[3]
    grad_ffn = gather_tokens(rms_back(branch_ffn, scale_ffn, cot_rows * gains[3]).astype(BF))
    grad_hidden = dot(grad_ffn, w_down)
    grad_gateup = jnp.concatenate(
        [grad_hidden * up_proj * slope, grad_hidden * activated], 1
    ).astype(BF)
    grad_mid = scatter_tokens(dot_last(grad_gateup, w_gateup))
    d_ffn = scatter_rows(
        jnp.concatenate([dot_first(normed_mid, grad_gateup), dot_first(grad_ffn, hidden_bf)], 1),
        z,
        xh,
    ).astype(BF)

    grad_resid = cot_rows + rms_back(hidden_in, scale_mid, gains[2] * grad_mid)
    grad_attn_own = rms_back(branch_attn, scale_attn, gains[1] * grad_resid).astype(BF)
    grad_attn = jnp.concatenate([grad_attn_own, send(grad_attn_own, "core", 1)], 0)
    grad_heads = dot(grad_attn, w_out).astype(BF)
    grad_probs = dot_last(grad_heads, vals)
    row_delta = jnp.sum(grad_heads.astype(F32) * attended, axis=-1, keepdims=True)
    grad_scores = (probs * (grad_probs - row_delta)).astype(BF)
    grad_qrot = dot(grad_scores, keys) * score_scale
    key_terms = dot_first(grad_scores, query_bf)
    val_terms = dot_first(probs_bf, grad_heads)
    kv_away = swap_halves(jnp.where(first, val_terms, key_terms).astype(BF))
    kv_terms = jnp.where(first, key_terms, val_terms) + send(kv_away, "core", 1).astype(F32)
    kv_rounded = kv_terms.astype(BF)
    kv_total = kv_terms[:chip_len]
    for k in range(1, 4):
        kv_total = kv_total + send(
            kv_rounded[k * chip_len : (k + 1) * chip_len], "y", -k
        ).astype(F32)
    grad_kvrot = pair_sum(kv_total)

    grad_qn = rotate_back(grad_qrot, cos_table, sin_table)
    grad_q_bf = rms_back(queries, scale_q, head_scale[0] * grad_qn).astype(BF)
    grad_kn = rotate_back(grad_kvrot, cos_table, sin_table)
    grad_k = rms_back(kv_raw, scale_k, head_scale[1] * grad_kn)
    grad_kv_bf = jnp.where(first, grad_k, grad_kvrot).astype(BF)
    d_qkv = dot_first(normed_in, jnp.concatenate([grad_q_bf, grad_kv_bf], 1))
    d_out = dot_first(grad_attn, attended_bf)
    d_attn = ring_sum(scatter_rows(jnp.concatenate([d_qkv, d_out], 1), z, xh).astype(BF))
    grad_norm_in = chip_scatter(
        dot_last(jnp.concatenate([grad_q_bf, grad_kv_bf * 0.5], 1), w_qkv)
    )
    grad_tokens = grad_resid + rms_back(tokens, scale_in, gains[0] * grad_norm_in)

    only_first = jnp.where(first, 0.5, 0.0)
    head_row = jnp.concatenate(
        [
            jnp.sum(unit_q * grad_qn, axis=0),
            only_first * jnp.sum(unit_k * grad_kn, axis=0),
            jnp.zeros((model_width - 2 * HD,), F32),
        ]
    )
    gain_rows = [
        jnp.sum(unit_in * grad_norm_in, axis=0),
        jnp.sum(unit_attn * grad_resid, axis=0),
        jnp.sum(unit_mid * grad_mid, axis=0),
        jnp.sum(unit_ffn * cot_rows, axis=0),
    ]
    small = small_sum(jnp.stack([0.5 * r for r in gain_rows] + [head_row]))
    d_head = small[4, : 2 * HD].reshape(2, HD)
    d_gains = lax.dynamic_slice(small, (0, (z * 2 + xh) * shard_rows), (4, shard_rows)).T

    d_attn_bf = d_attn.astype(BF)
    d_other = send(d_attn_bf, "core", 1)
    by_core = jnp.where(
        first, jnp.stack([d_attn_bf, d_other], 1), jnp.stack([d_other, d_attn_bf], 1)
    ).astype(F32)
    d_split = jnp.stack(
        [
            by_core[:, :, :HD].reshape(shard_rows, 2 * HD),
            by_core[:, :, 2 * HD :].reshape(shard_rows, 2 * HD),
        ],
        1,
    )
    d_shared = by_core[:, :, HD : 2 * HD]

    mine = [d_ffn] + [send(d_ffn, "y", k) for k in range(1, 4)]
    mine = jnp.stack(mine)
    other = send(mine, "core", 1)
    both = jnp.where(first, jnp.stack([mine, other], 1), jnp.stack([other, mine], 1))
    twice = jnp.concatenate([both[::-1], both[::-1]], 0)
    ordered = lax.dynamic_slice_in_dim(twice, 3 - y, 4, 0)
    ordered = ordered.reshape(8, shard_rows, 3, ff_pad)[..., :ff_local]
    d_all = ordered.transpose(1, 2, 0, 3).reshape(shard_rows, 3, 8 * ff_local).astype(F32)
    return (
        result[None],
        grad_tokens[None],
        d_gains,
        d_head,
        d_split,
        d_shared,
        d_all[:, :2],
        d_all[:, 2],
    )


def solution(mesh):
    fine = Mesh(mesh.devices.reshape(4, 2, 4, 2, 2), ("z", "xh", "y", "core", "tp"))
    fsdp, ctx, tp = ("z", "xh"), ("y", "core"), "tp"
    in_specs = (
        P(fsdp, ctx, None),
        P(fsdp, ctx),
        P(fsdp, None),
        P(),
        P(fsdp, None, tp),
        P(fsdp, None, None),
        P(fsdp, None, tp),
        P(fsdp, tp),
        P(fsdp, ctx, None),
    )
    out_specs = (
        P(fsdp, ctx, None),
        P(fsdp, ctx, None),
        P(fsdp, None),
        P(),
        P(fsdp, None, tp),
        P(fsdp, None, None),
        P(fsdp, None, tp),
        P(fsdp, tp),
    )
    return jax.shard_map(
        on_device, mesh=fine, in_specs=in_specs, out_specs=out_specs, check_vma=False
    )
```

```python
import jax
import jax.numpy as jnp
from jax import lax
from jax.experimental import pallas as pl
from jax.experimental.pallas import tpu as pltpu
from jax.sharding import Mesh, PartitionSpec as P

HD = 256
EPSILON = 1e-06
ROPE_BASE = 1000000.0
MASKED_SCORE = -1e30
SIZE = {"z": 4, "xh": 2, "y": 4, "core": 2, "tp": 2}
BF = jnp.bfloat16
F32 = jnp.float32


def inv_rms(values):
    return lax.rsqrt(jnp.mean(values * values, axis=-1, keepdims=True) + EPSILON)


def rms_back(values, scale_rows, cot_scaled):
    return scale_rows * cot_scaled - values * scale_rows**3 * jnp.mean(
        values * cot_scaled, axis=-1, keepdims=True
    )


def rotate(values, cos_table, sin_table):
    middle = values.shape[-1] // 2
    upper_half = values[..., :middle]
    lower_half = values[..., middle:]
    return jnp.concatenate(
        [
            upper_half * cos_table - lower_half * sin_table,
            lower_half * cos_table + upper_half * sin_table,
        ],
        axis=-1,
    )


def rotate_back(values, cos_table, sin_table):
    return rotate(values, cos_table, -sin_table)


def dot(left, right):
    return jnp.dot(left, right, preferred_element_type=F32)


def dot_last(left, right):
    return lax.dot_general(left, right, (((1,), (1,)), ((), ())), preferred_element_type=F32)


def dot_first(left, right):
    return lax.dot_general(left, right, (((0,), (0,)), ((), ())), preferred_element_type=F32)


def send(array, axis, shift):
    n = SIZE[axis]
    return lax.ppermute(array, axis, [(i, (i + shift) % n) for i in range(n)])


def tie(value, late):
    return lax.optimization_barrier((value, late))[0]


def put(whole, block, index):
    start = (index,) + (0,) * (whole.ndim - 1)
    return lax.dynamic_update_slice(whole, block[None], start, allow_negative_indices=False)


def pick(array, index):
    start = (index,) + (0,) * (array.ndim - 1)
    return lax.dynamic_slice(array, start, (1,) + array.shape[1:], allow_negative_indices=False)[0]


def ordered_pair(own, other, place):
    first = jnp.concatenate([own, other], 0)
    return jnp.where(place == 0, first, jnp.concatenate([other, own], 0))


def gather_rows(shard, z, xh, late=None):
    rows = shard.shape[0]
    pair = ordered_pair(shard, send(shard, "xh", 1), xh)
    if late is not None:
        pair = tie(pair, late)
    whole = put(jnp.zeros((4,) + pair.shape, shard.dtype), pair, z)
    for k in (1, 3, 2):
        whole = put(whole, send(pair, "z", k), (z - k) & 3)
    return whole.reshape((8 * rows,) + shard.shape[1:])


def scatter_rows(whole, z, xh, late_z=None, late_xh=None):
    total, cols = whole.shape
    rows = total // 8
    blocks = whole.astype(BF).reshape(4, 2 * rows, cols)
    got = [send(pick(blocks, (z - k) & 3), "z", -k) for k in (1, 3, 2)]
    pair = pick(blocks, z)
    if late_z is not None:
        got, pair = tie((got, pair), late_z)
    pair = pair.astype(F32)
    for part in got:
        pair = pair + part.astype(F32)
    pair = pair.reshape(2, rows, cols)
    away = send(pick(pair, 1 - xh).astype(BF), "xh", 1)
    own = pick(pair, xh)
    if late_xh is not None:
        own, away = tie((own, away), late_xh)
    return own + away.astype(F32)


def assemble(mine, other, place):
    rows, cols = mine.shape[1:]
    slot = cols // 3
    step = 16
    full = 27 * 128

    def kernel(place_ref, mine_ref, other_ref, gu_ref, down_ref):
        for c in range(8):
            from_y, from_core = c // 2, c % 2
            k = (place_ref[0] - from_y) & 3
            block = jnp.where(place_ref[1] == from_core, mine_ref[k], other_ref[k]).astype(F32)
            start = min(4 * c, 3 * c + 3) * 128
            width = (4 if c < 3 else 3) * 128
            skip = 128 if c == 7 else 0
            lanes = slice(start, start + width)
            gu_ref[:, 0, lanes] = block[:, skip : skip + width]
            gu_ref[:, 1, lanes] = block[:, slot + skip : slot + skip + width]
            down_ref[:, lanes] = block[:, 2 * slot + skip : 2 * slot + skip + width]

    return pl.pallas_call(
        kernel,
        out_shape=(
            jax.ShapeDtypeStruct((rows, 2, full), F32),
            jax.ShapeDtypeStruct((rows, full), F32),
        ),
        grid_spec=pltpu.PrefetchScalarGridSpec(
            num_scalar_prefetch=1,
            grid=(rows // step,),
            in_specs=[pl.BlockSpec((4, step, cols), lambda i, p: (0, i, 0))] * 2,
            out_specs=[
                pl.BlockSpec((step, 2, full), lambda i, p: (i, 0, 0)),
                pl.BlockSpec((step, full), lambda i, p: (i, 0)),
            ],
        ),
    )(place, mine, other)


def by_distance(block):
    got = {k: send(block, "y", k) for k in (1, 3, 2)}
    return [block, got[1], got[2], got[3]]


def gather_tokens(block):
    mine = jnp.concatenate(by_distance(block), 0)
    return jnp.concatenate([mine, send(mine, "core", 1)], 0)


def pair_sum(array):
    rounded = array.astype(BF)
    return rounded.astype(F32) + send(rounded, "tp", 1).astype(F32)


def scatter_y(mine):
    local = mine.shape[0] // 4
    rounded = mine.astype(BF)
    total = mine[:local]
    for k in (1, 3, 2):
        total = total + send(rounded[k * local : (k + 1) * local], "y", -k).astype(F32)
    return total, rounded


def scatter_tokens(partial):
    half = partial.shape[0] // 2
    away = send(partial[half:].astype(BF), "core", 1)
    total, sent = scatter_y(partial[:half] + away.astype(F32))
    return pair_sum(total), sent


def ring_sum(array):
    got = [send(array, "y", k).astype(F32) for k in (1, 2, 3)]
    return (array.astype(F32) + got[1]) + (got[0] + got[2])


def small_sum(array):
    array = array + send(array, "core", 1)
    array = array + send(array, "tp", 1)
    array = array + send(array, "xh", 1)
    for axis in ("y", "z"):
        got = [send(array, axis, k) for k in range(1, 4)]
        array = (array + got[1]) + (got[0] + got[2])
    return array


def swap_halves(array):
    rows, cols = array.shape
    half = 128
    parts = array.reshape(rows // (2 * half), 2, half, cols)
    return jnp.concatenate([parts[:, 1:], parts[:, :1]], 1).reshape(rows, cols)


def on_device(
    inputs,
    positions,
    norm_gains,
    head_gains,
    attn_split,
    attn_shared,
    ffn_gate_up,
    ffn_down,
    cotangent,
):
    z, xh, y, core = (lax.axis_index(a) for a in ("z", "xh", "y", "core"))
    first = core == 0
    tokens = inputs[0]
    cot_rows = cotangent[0]
    local_len, model_width = tokens.shape
    shard_rows = attn_split.shape[0]
    ff_pad = 512
    place = y * 2 + core
    block_start = jnp.minimum(jnp.minimum(4 * place, 3 * place + 3), 23)

    def cut(array, start, sizes):
        return lax.dynamic_slice(array, start, sizes, allow_negative_indices=False)

    gains_wide = jnp.pad(norm_gains.T, ((0, 4), (0, 0)))[None]
    gains = gather_rows(gains_wide, z, xh).transpose(1, 0, 2).reshape(8, model_width).astype(F32)
    wq_shard = cut(attn_split, (0, 0, core * HD), (shard_rows, 1, HD))[:, 0]
    wo_shard = cut(attn_split, (0, 1, core * HD), (shard_rows, 1, HD))[:, 0]
    wkv_shard = cut(attn_shared, (0, core, 0), (shard_rows, 1, HD))[:, 0]
    w_qkv = gather_rows(jnp.concatenate([wq_shard, wkv_shard], 1), z, xh)
    w_out = gather_rows(wo_shard, z, xh, w_qkv)
    gu_shard = cut(ffn_gate_up, (0, 0, block_start * 128), (shard_rows, 2, ff_pad))
    down_shard = cut(ffn_down, (0, block_start * 128), (shard_rows, ff_pad))
    slot = jnp.arange(ff_pad, dtype=jnp.int32) // 128
    used = (slot < jnp.where(place < 3, 4, 3) + (place == 7)) & (slot >= (place == 7))
    gate_shard = jnp.where(used[None], gu_shard[:, 0], jnp.zeros((), BF))
    ffn_all = gather_rows(
        jnp.concatenate([gate_shard, gu_shard[:, 1], down_shard], 1), z, xh, w_qkv
    )
    w_gateup = ffn_all[:, : 2 * ff_pad]
    w_down = ffn_all[:, 2 * ff_pad :]

    head_scale = head_gains.astype(F32)
    score_scale = HD ** (-0.5)
    frequency = ROPE_BASE ** (-2.0 * jnp.arange(HD // 2, dtype=F32) / HD)
    own_pos = positions.astype(F32)
    chip_pos = jnp.concatenate([own_pos, send(own_pos, "core", 1)], 1)[0]
    angles = chip_pos[:, None] * frequency[None, :]
    cos_table = jnp.cos(angles)
    sin_table = jnp.sin(angles)

    scale_in = inv_rms(tokens)
    unit_in = tokens * scale_in
    normed_own = (unit_in * gains[0]).astype(BF)
    normed_in = jnp.concatenate([normed_own, send(normed_own, "core", 1)], 0)
    qkv = dot(normed_in, w_qkv)
    queries = qkv[:, :HD]
    kv_raw = qkv[:, HD:]
    scale_q = inv_rms(queries)
    unit_q = queries * scale_q
    scale_k = inv_rms(kv_raw)
    unit_k = kv_raw * scale_k
    query_bf = (rotate(unit_q * head_scale[0], cos_table, sin_table) * score_scale).astype(BF)
    kv_bf = jnp.where(first, rotate(unit_k * head_scale[1], cos_table, sin_table), kv_raw).astype(
        BF
    )
    kv_mine = jnp.concatenate(by_distance(kv_bf), 0)
    kv_other = swap_halves(send(kv_mine, "core", 1))
    keys = jnp.where(first, kv_mine, kv_other)
    vals = jnp.where(first, kv_other, kv_mine)

    chip_len = 2 * local_len
    seq_len = 4 * chip_len
    q_iota = jnp.arange(chip_len, dtype=jnp.int32)
    q_core = (core + (q_iota >> 7)) & 1
    query_index = y * chip_len + q_core * local_len + (q_iota & 127)
    k_iota = jnp.arange(seq_len, dtype=jnp.int32)
    k_core = (core + (k_iota >> 7)) & 1
    key_index = ((y - (k_iota >> 8)) & 3) * chip_len + k_core * local_len + (k_iota & 127)
    begin = query_index - chip_pos.astype(jnp.int32)
    visible = (key_index[None, :] <= query_index[:, None]) & (key_index[None, :] >= begin[:, None])
    scores = jnp.where(visible, dot_last(query_bf, keys), MASKED_SCORE)
    row_max = jnp.max(scores, axis=-1, keepdims=True)
    log_total = row_max + jnp.log(jnp.sum(jnp.exp(scores - row_max), axis=-1, keepdims=True))
    probs = jnp.exp(scores - log_total)
    probs_bf = probs.astype(BF)
    attended = dot(probs_bf, vals)
    attended_bf = attended.astype(BF)

    def chip_scatter(partial):
        away = send(partial[local_len:].astype(BF), "core", 1)
        return pair_sum(partial[:local_len] + away.astype(F32))

    branch_attn = chip_scatter(dot_last(attended_bf, w_out))
    scale_attn = inv_rms(branch_attn)
    unit_attn = branch_attn * scale_attn
    hidden_in = tokens + unit_attn * gains[1]
    scale_mid = inv_rms(hidden_in)
    unit_mid = hidden_in * scale_mid
    normed_mid = gather_tokens((unit_mid * gains[2]).astype(BF))

    gate_up = dot(normed_mid, w_gateup)
    gate_pre = gate_up[:, :ff_pad]
    up_proj = gate_up[:, ff_pad:]
    cube = 0.7978845608028654
    tanh_part = jnp.tanh(cube * (gate_pre + 0.044715 * gate_pre**3))
    activated = 0.5 * gate_pre * (1.0 + tanh_part)
    slope = 0.5 * (1.0 + tanh_part) + 0.5 * gate_pre * (1.0 - tanh_part * tanh_part) * cube * (
        1.0 + 3.0 * 0.044715 * gate_pre * gate_pre
    )
    hidden_bf = (activated * up_proj).astype(BF)
    branch_ffn, _ = scatter_tokens(dot_last(hidden_bf, w_down))
    scale_ffn = inv_rms(branch_ffn)
    unit_ffn = branch_ffn * scale_ffn
    result = hidden_in + unit_ffn * gains[3]
    grad_ffn = gather_tokens(rms_back(branch_ffn, scale_ffn, cot_rows * gains[3]).astype(BF))
    grad_hidden = dot(grad_ffn, w_down)
    grad_gateup = jnp.concatenate(
        [grad_hidden * up_proj * slope, grad_hidden * activated], 1
    ).astype(BF)
    grad_mid, sent = scatter_tokens(dot_last(grad_gateup, w_gateup))
    late_mid, late_gateup, late_ffn, late_hidden = tie(
        (normed_mid, grad_gateup, grad_ffn, hidden_bf), sent
    )
    d_ffn_all = jnp.concatenate(
        [dot_first(late_mid, late_gateup), dot_first(late_ffn, late_hidden)], 1
    )

    grad_resid = cot_rows + rms_back(hidden_in, scale_mid, gains[2] * grad_mid)
    grad_attn_own = rms_back(branch_attn, scale_attn, gains[1] * grad_resid).astype(BF)
    grad_attn = jnp.concatenate([grad_attn_own, send(grad_attn_own, "core", 1)], 0)
    grad_heads = dot(grad_attn, w_out).astype(BF)
    grad_probs = dot_last(grad_heads, vals)
    row_delta = jnp.sum(grad_heads.astype(F32) * attended, axis=-1, keepdims=True)
    grad_scores = (probs * (grad_probs - row_delta)).astype(BF)
    grad_qrot = dot(grad_scores, keys) * score_scale
    key_terms = dot_first(grad_scores, query_bf)
    val_terms = dot_first(probs_bf, grad_heads)
    kv_away = swap_halves(jnp.where(first, val_terms, key_terms).astype(BF))
    kv_terms = jnp.where(first, key_terms, val_terms) + send(kv_away, "core", 1).astype(F32)
    kv_total, kv_sent = scatter_y(kv_terms)
    grad_kvrot = pair_sum(kv_total)
    d_ffn = scatter_rows(d_ffn_all, z, xh, kv_sent, grad_kvrot).astype(BF)

    grad_qn = rotate_back(grad_qrot, cos_table, sin_table)
    grad_q_bf = rms_back(queries, scale_q, head_scale[0] * grad_qn).astype(BF)
    grad_kn = rotate_back(grad_kvrot, cos_table, sin_table)
    grad_k = rms_back(kv_raw, scale_k, head_scale[1] * grad_kn)
    grad_kv_bf = jnp.where(first, grad_k, grad_kvrot).astype(BF)
    d_early = jnp.concatenate(
        [dot_first(normed_in, grad_q_bf), dot_first(grad_attn, attended_bf)], 1
    )
    d_early = ring_sum(scatter_rows(d_early, z, xh).astype(BF)).astype(BF)
    d_late = ring_sum(scatter_rows(dot_first(normed_in, grad_kv_bf), z, xh).astype(BF)).astype(BF)
    partial_in = dot_last(jnp.concatenate([grad_q_bf, grad_kv_bf * 0.5], 1), w_qkv)
    grad_norm_in = chip_scatter(partial_in)
    grad_tokens = grad_resid + rms_back(tokens, scale_in, gains[0] * grad_norm_in)

    only_first = jnp.where(first, 0.5, 0.0)
    head_row = jnp.concatenate(
        [
            jnp.sum(unit_q * grad_qn, axis=0),
            only_first * jnp.sum(unit_k * grad_kn, axis=0),
            jnp.zeros((model_width - 2 * HD,), F32),
        ]
    )
    gain_rows = [
        2.0 * jnp.sum(normed_in.astype(F32) * partial_in, axis=0) / gains[0],
        jnp.sum(unit_attn * grad_resid, axis=0),
        jnp.sum(unit_mid * grad_mid, axis=0),
        jnp.sum(unit_ffn * cot_rows, axis=0),
    ]
    small = small_sum(jnp.stack([0.5 * r for r in gain_rows] + [head_row]))
    d_head = small[4, : 2 * HD].reshape(2, HD)
    d_gains = cut(small, (0, (z * 2 + xh) * shard_rows), (4, shard_rows)).T

    def join(own, axis):
        other = send(own, "core", 1)
        lead = jnp.stack([own, other], axis)
        return jnp.where(first, lead, jnp.stack([other, own], axis)).astype(F32)

    early = join(d_early, 1)
    d_split = jnp.stack(
        [early[:, :, :HD].reshape(shard_rows, 2 * HD), early[:, :, HD:].reshape(shard_rows, 2 * HD)],
        1,
    )
    d_shared = join(d_late, 1)
    mine = jnp.stack(by_distance(d_ffn))
    d_gate_up, d_down = assemble(mine, send(mine, "core", 1), jnp.stack([y, core]))
    return (
        result[None],
        grad_tokens[None],
        d_gains,
        d_head,
        d_split,
        d_shared,
        d_gate_up,
        d_down,
    )


def solution(mesh):
    fine = Mesh(mesh.devices.reshape(4, 2, 4, 2, 2), ("z", "xh", "y", "core", "tp"))
    fsdp, ctx, tp = ("z", "xh"), ("y", "core"), "tp"
    in_specs = (
        P(fsdp, ctx, None),
        P(fsdp, ctx),
        P(fsdp, None),
        P(),
        P(fsdp, None, tp),
        P(fsdp, None, None),
        P(fsdp, None, tp),
        P(fsdp, tp),
        P(fsdp, ctx, None),
    )
    out_specs = (
        P(fsdp, ctx, None),
        P(fsdp, ctx, None),
        P(fsdp, None),
        P(),
        P(fsdp, None, tp),
        P(fsdp, None, None),
        P(fsdp, None, tp),
        P(fsdp, tp),
    )
    return jax.shard_map(
        on_device, mesh=fine, in_specs=in_specs, out_specs=out_specs, check_vma=False
    )
```

```python
import jax
import jax.numpy as jnp
from jax import lax
from jax.experimental import pallas as pl
from jax.experimental.pallas import tpu as pltpu
from jax.sharding import Mesh, PartitionSpec as P

HD = 256
EPSILON = 1e-06
ROPE_BASE = 1000000.0
MASKED_SCORE = -1e30
SIZE = {"z": 4, "xh": 2, "y": 4, "core": 2, "tp": 2}
BF = jnp.bfloat16
F32 = jnp.float32


def inv_rms(values):
    return lax.rsqrt(jnp.mean(values * values, axis=-1, keepdims=True) + EPSILON)


def rms_back(values, scale_rows, cot_scaled):
    return scale_rows * cot_scaled - values * scale_rows**3 * jnp.mean(
        values * cot_scaled, axis=-1, keepdims=True
    )


def rotate(values, cos_table, sin_table):
    middle = values.shape[-1] // 2
    upper_half = values[..., :middle]
    lower_half = values[..., middle:]
    return jnp.concatenate(
        [
            upper_half * cos_table - lower_half * sin_table,
            lower_half * cos_table + upper_half * sin_table,
        ],
        axis=-1,
    )


def rotate_back(values, cos_table, sin_table):
    return rotate(values, cos_table, -sin_table)


def dot(left, right):
    return jnp.dot(left, right, preferred_element_type=F32)


def dot_last(left, right):
    return lax.dot_general(left, right, (((1,), (1,)), ((), ())), preferred_element_type=F32)


def dot_first(left, right):
    return lax.dot_general(left, right, (((0,), (0,)), ((), ())), preferred_element_type=F32)


def send(array, axis, shift):
    n = SIZE[axis]
    return lax.ppermute(array, axis, [(i, (i + shift) % n) for i in range(n)])


def tie(value, late):
    return lax.optimization_barrier((value, late))[0]


def put(whole, block, index):
    start = (index,) + (0,) * (whole.ndim - 1)
    return lax.dynamic_update_slice(whole, block[None], start, allow_negative_indices=False)


def pick(array, index):
    start = (index,) + (0,) * (array.ndim - 1)
    return lax.dynamic_slice(array, start, (1,) + array.shape[1:], allow_negative_indices=False)[0]


def ordered_pair(own, other, place):
    first = jnp.concatenate([own, other], 0)
    return jnp.where(place == 0, first, jnp.concatenate([other, own], 0))


def gather_rows(shard, z, xh, late=None):
    rows = shard.shape[0]
    pair = ordered_pair(shard, send(shard, "xh", 1), xh)
    if late is not None:
        pair = tie(pair, late)
    whole = put(jnp.zeros((4,) + pair.shape, shard.dtype), pair, z)
    for k in (1, 3, 2):
        whole = put(whole, send(pair, "z", k), (z - k) & 3)
    return whole.reshape((8 * rows,) + shard.shape[1:])


def scatter_rows(blocks, z, xh, late_z=None, late_xh=None):
    got = [send(pick(blocks, (z - k) & 3), "z", -k) for k in (1, 2, 3)]
    own = pick(blocks, z)
    if late_z is not None:
        got, own = tie((got, own), late_z)
    one, two, three = (part.astype(F32) for part in got)
    pair = ((own.astype(F32) + two) + (one + three)).astype(BF)
    away = send(pick(pair, 1 - xh), "xh", 1)
    own = pick(pair, xh)
    if late_xh is not None:
        own, away = tie((own, away), late_xh)
    return own.astype(F32) + away.astype(F32)


def in_blocks(whole):
    rows, cols = whole.shape
    return whole.astype(BF).reshape(4, 2, rows // 8, cols)


def assemble(mine, other, place):
    rows, cols = mine.shape[1:]
    slot = cols // 3
    step = 16
    full = 27 * 128

    def kernel(place_ref, mine_ref, other_ref, gu_ref, down_ref):
        for c in range(8):
            from_y, from_core = c // 2, c % 2
            k = (place_ref[0] - from_y) & 3
            block = jnp.where(place_ref[1] == from_core, mine_ref[k], other_ref[k]).astype(F32)
            start = min(4 * c, 3 * c + 3) * 128
            width = (4 if c < 3 else 3) * 128
            skip = 128 if c == 7 else 0
            lanes = slice(start, start + width)
            gu_ref[:, 0, lanes] = block[:, skip : skip + width]
            gu_ref[:, 1, lanes] = block[:, slot + skip : slot + skip + width]
            down_ref[:, lanes] = block[:, 2 * slot + skip : 2 * slot + skip + width]

    return pl.pallas_call(
        kernel,
        out_shape=(
            jax.ShapeDtypeStruct((rows, 2, full), F32),
            jax.ShapeDtypeStruct((rows, full), F32),
        ),
        grid_spec=pltpu.PrefetchScalarGridSpec(
            num_scalar_prefetch=1,
            grid=(rows // step,),
            in_specs=[pl.BlockSpec((4, step, cols), lambda i, p: (0, i, 0))] * 2,
            out_specs=[
                pl.BlockSpec((step, 2, full), lambda i, p: (i, 0, 0)),
                pl.BlockSpec((step, full), lambda i, p: (i, 0)),
            ],
        ),
    )(place, mine, other)


def by_distance(block):
    got = {k: send(block, "y", k) for k in (1, 3, 2)}
    return [block, got[1], got[2], got[3]]


def gather_tokens(block):
    mine = jnp.concatenate(by_distance(block), 0)
    return jnp.concatenate([mine, send(mine, "core", 1)], 0)


def pair_sum(array):
    rounded = array.astype(BF)
    return rounded.astype(F32) + send(rounded, "tp", 1).astype(F32)


def scatter_y(mine):
    local = mine.shape[0] // 4
    rounded = mine.astype(BF)
    total = mine[:local]
    for k in (1, 3, 2):
        total = total + send(rounded[k * local : (k + 1) * local], "y", -k).astype(F32)
    return total, rounded


def scatter_tokens(partial):
    half = partial.shape[0] // 2
    away = send(partial[half:].astype(BF), "core", 1)
    total, sent = scatter_y(partial[:half] + away.astype(F32))
    return pair_sum(total), sent


def ring_sum(array):
    got = [send(array, "y", k).astype(F32) for k in (1, 2, 3)]
    return (array.astype(F32) + got[1]) + (got[0] + got[2])


def swap_halves(array):
    rows, cols = array.shape
    half = 128
    parts = array.reshape(rows // (2 * half), 2, half, cols)
    return jnp.concatenate([parts[:, 1:], parts[:, :1]], 1).reshape(rows, cols)


def on_device(
    inputs,
    positions,
    norm_gains,
    head_gains,
    attn_split,
    attn_shared,
    ffn_gate_up,
    ffn_down,
    cotangent,
):
    z, xh, y, core = (lax.axis_index(a) for a in ("z", "xh", "y", "core"))
    first = core == 0
    tokens = inputs[0]
    cot_rows = cotangent[0]
    local_len, model_width = tokens.shape
    shard_rows = attn_split.shape[0]
    ff_pad = 512
    place = y * 2 + core
    block_start = jnp.minimum(jnp.minimum(4 * place, 3 * place + 3), 23)

    def cut(array, start, sizes):
        return lax.dynamic_slice(array, start, sizes, allow_negative_indices=False)

    wq_shard = cut(attn_split, (0, 0, core * HD), (shard_rows, 1, HD))[:, 0]
    wo_shard = cut(attn_split, (0, 1, core * HD), (shard_rows, 1, HD))[:, 0]
    wkv_shard = cut(attn_shared, (0, core, 0), (shard_rows, 1, HD))[:, 0]
    gains_shard = jnp.pad(norm_gains, ((0, 0), (0, 124)))
    attn_all = gather_rows(
        jnp.concatenate([wq_shard, wkv_shard, wo_shard, gains_shard], 1), z, xh
    )
    w_qkv = attn_all[:, : 2 * HD]
    w_out = attn_all[:, 2 * HD : 3 * HD]
    gains = attn_all[:, 3 * HD : 3 * HD + 8].T.astype(F32)
    gu_shard = cut(ffn_gate_up, (0, 0, block_start * 128), (shard_rows, 2, ff_pad))
    down_shard = cut(ffn_down, (0, block_start * 128), (shard_rows, ff_pad))
    slot = jnp.arange(ff_pad, dtype=jnp.int32) // 128
    used = (slot < jnp.where(place < 3, 4, 3) + (place == 7)) & (slot >= (place == 7))
    gate_shard = jnp.where(used[None], gu_shard[:, 0], jnp.zeros((), BF))
    head_scale = head_gains.astype(F32)
    score_scale = HD ** (-0.5)
    frequency = ROPE_BASE ** (-2.0 * jnp.arange(HD // 2, dtype=F32) / HD)
    own_pos = positions.astype(F32)
    chip_pos = jnp.concatenate([own_pos, send(own_pos, "core", 1)], 1)[0]
    angles = chip_pos[:, None] * frequency[None, :]
    cos_table = jnp.cos(angles)
    sin_table = jnp.sin(angles)

    scale_in = inv_rms(tokens)
    unit_in = tokens * scale_in
    normed_own = (unit_in * gains[0]).astype(BF)
    normed_in = jnp.concatenate([normed_own, send(normed_own, "core", 1)], 0)
    qkv = dot(normed_in, w_qkv)
    queries = qkv[:, :HD]
    kv_raw = qkv[:, HD:]
    scale_q = inv_rms(queries)
    unit_q = queries * scale_q
    scale_k = inv_rms(kv_raw)
    unit_k = kv_raw * scale_k
    query_bf = (rotate(unit_q * head_scale[0], cos_table, sin_table) * score_scale).astype(BF)
    kv_bf = jnp.where(first, rotate(unit_k * head_scale[1], cos_table, sin_table), kv_raw).astype(
        BF
    )
    kv_mine = jnp.concatenate(by_distance(kv_bf), 0)
    ffn_all = gather_rows(
        jnp.concatenate([gate_shard, gu_shard[:, 1], down_shard], 1), z, xh, kv_bf
    )
    w_gateup = ffn_all[:, : 2 * ff_pad]
    w_down = ffn_all[:, 2 * ff_pad :]
    kv_other = swap_halves(send(kv_mine, "core", 1))
    keys = jnp.where(first, kv_mine, kv_other)
    vals = jnp.where(first, kv_other, kv_mine)

    chip_len = 2 * local_len
    seq_len = 4 * chip_len
    q_iota = jnp.arange(chip_len, dtype=jnp.int32)
    q_core = (core + (q_iota >> 7)) & 1
    query_index = y * chip_len + q_core * local_len + (q_iota & 127)
    k_iota = jnp.arange(seq_len, dtype=jnp.int32)
    k_core = (core + (k_iota >> 7)) & 1
    key_index = ((y - (k_iota >> 8)) & 3) * chip_len + k_core * local_len + (k_iota & 127)
    begin = query_index - chip_pos.astype(jnp.int32)
    visible = (key_index[None, :] <= query_index[:, None]) & (key_index[None, :] >= begin[:, None])
    scores = jnp.where(visible, dot_last(query_bf, keys), MASKED_SCORE)
    row_max = jnp.max(scores, axis=-1, keepdims=True)
    log_total = row_max + jnp.log(jnp.sum(jnp.exp(scores - row_max), axis=-1, keepdims=True))
    probs = jnp.exp(scores - log_total)
    probs_bf = probs.astype(BF)
    attended = dot(probs_bf, vals)
    attended_bf = attended.astype(BF)

    def chip_scatter(partial):
        away = send(partial[local_len:].astype(BF), "core", 1)
        return pair_sum(partial[:local_len] + away.astype(F32))

    branch_attn = chip_scatter(dot_last(attended_bf, w_out))
    scale_attn = inv_rms(branch_attn)
    unit_attn = branch_attn * scale_attn
    hidden_in = tokens + unit_attn * gains[1]
    scale_mid = inv_rms(hidden_in)
    unit_mid = hidden_in * scale_mid
    normed_mid = gather_tokens((unit_mid * gains[2]).astype(BF))

    gate_up = dot(normed_mid, w_gateup)
    gate_pre = gate_up[:, :ff_pad]
    up_proj = gate_up[:, ff_pad:]
    cube = 0.7978845608028654
    tanh_part = jnp.tanh(cube * (gate_pre + 0.044715 * gate_pre**3))
    activated = 0.5 * gate_pre * (1.0 + tanh_part)
    slope = 0.5 * (1.0 + tanh_part) + 0.5 * gate_pre * (1.0 - tanh_part * tanh_part) * cube * (
        1.0 + 3.0 * 0.044715 * gate_pre * gate_pre
    )
    hidden_bf = (activated * up_proj).astype(BF)
    branch_ffn, _ = scatter_tokens(dot_last(hidden_bf, w_down))
    scale_ffn = inv_rms(branch_ffn)
    unit_ffn = branch_ffn * scale_ffn
    result = hidden_in + unit_ffn * gains[3]
    grad_ffn = gather_tokens(rms_back(branch_ffn, scale_ffn, cot_rows * gains[3]).astype(BF))
    grad_hidden = dot(grad_ffn, w_down)
    grad_gateup = jnp.concatenate(
        [grad_hidden * up_proj * slope, grad_hidden * activated], 1
    ).astype(BF)
    grad_mid, sent = scatter_tokens(dot_last(grad_gateup, w_gateup))
    late_mid, late_gateup, late_ffn, late_hidden = tie(
        (normed_mid, grad_gateup, grad_ffn, hidden_bf), sent
    )
    d_ffn_all = jnp.concatenate(
        [dot_first(late_mid, late_gateup), dot_first(late_ffn, late_hidden)], 1
    )

    grad_resid = cot_rows + rms_back(hidden_in, scale_mid, gains[2] * grad_mid)
    grad_attn_own = rms_back(branch_attn, scale_attn, gains[1] * grad_resid).astype(BF)
    grad_attn = jnp.concatenate([grad_attn_own, send(grad_attn_own, "core", 1)], 0)
    grad_heads = dot(grad_attn, w_out).astype(BF)
    grad_probs = dot_last(grad_heads, vals)
    row_delta = jnp.sum(grad_heads.astype(F32) * attended, axis=-1, keepdims=True)
    grad_scores = (probs * (grad_probs - row_delta)).astype(BF)
    grad_qrot = dot(grad_scores, keys) * score_scale
    key_terms = dot_first(grad_scores, query_bf)
    val_terms = dot_first(probs_bf, grad_heads)
    kv_away = swap_halves(jnp.where(first, val_terms, key_terms).astype(BF))
    kv_terms = jnp.where(first, key_terms, val_terms) + send(kv_away, "core", 1).astype(F32)
    kv_total, _ = scatter_y(kv_terms)
    grad_kvrot = pair_sum(kv_total)
    d_ffn = scatter_rows(in_blocks(d_ffn_all), z, xh, kv_total, grad_kvrot).astype(BF)

    grad_qn = rotate_back(grad_qrot, cos_table, sin_table)
    grad_q_bf = rms_back(queries, scale_q, head_scale[0] * grad_qn).astype(BF)
    grad_kn = rotate_back(grad_kvrot, cos_table, sin_table)
    grad_k = rms_back(kv_raw, scale_k, head_scale[1] * grad_kn)
    grad_kv_bf = jnp.where(first, grad_k, grad_kvrot).astype(BF)
    d_early = scatter_rows(
        in_blocks(
            jnp.concatenate(
                [dot_first(normed_in, grad_q_bf), dot_first(grad_attn, attended_bf)], 1
            )
        ),
        z,
        xh,
        grad_kvrot,
    ).astype(BF)
    partial_in = dot_last(jnp.concatenate([grad_q_bf, grad_kv_bf * 0.5], 1), w_qkv)
    grad_norm_in = chip_scatter(partial_in)
    grad_tokens = grad_resid + rms_back(tokens, scale_in, gains[0] * grad_norm_in)

    gain_rows = jnp.stack(
        [
            jnp.sum(normed_in.astype(F32) * partial_in, axis=0),
            0.5 * jnp.sum(unit_attn * grad_resid, axis=0),
            0.5 * jnp.sum(unit_mid * grad_mid, axis=0),
            0.5 * jnp.sum(unit_ffn * cot_rows, axis=0),
        ]
    )
    head_rows = jnp.stack(
        [
            jnp.sum(unit_q * grad_qn, axis=0),
            jnp.where(first, 0.5, 0.0) * jnp.sum(unit_k * grad_kn, axis=0),
        ]
    )
    gain_cols = jnp.pad(gain_rows.T, ((0, 0), (0, 124)))
    late = in_blocks(jnp.concatenate([dot_first(normed_in, grad_kv_bf), gain_cols], 1))
    head_block = jnp.pad(head_rows.astype(BF), ((0, 14), (0, 128)))
    late = jnp.concatenate([late, jnp.broadcast_to(head_block, (4, 2) + head_block.shape)], 2)
    d_late = scatter_rows(late, z, xh).astype(BF)
    d_attn = jnp.concatenate([jnp.pad(d_early, ((0, 16), (0, 0))), d_late], 1)
    d_attn = ring_sum(d_attn).astype(BF)
    other = send(d_attn, "core", 1)
    low = jnp.where(first, d_attn, other).astype(F32)
    high = jnp.where(first, other, d_attn).astype(F32)
    part = (low + high)[:, 2 * HD :]
    small = pair_sum(part)
    d_head = small[shard_rows : shard_rows + 2, :HD]
    d_gains = small[:shard_rows, HD : HD + 4]
    d_gains = jnp.concatenate(
        [d_gains[:, :1] / norm_gains[:, :1].astype(F32), d_gains[:, 1:]], 1
    )
    low, high = low[:shard_rows], high[:shard_rows]
    d_split = jnp.stack(
        [
            jnp.concatenate([low[:, :HD], high[:, :HD]], 1),
            jnp.concatenate([low[:, HD : 2 * HD], high[:, HD : 2 * HD]], 1),
        ],
        1,
    )
    d_shared = jnp.stack([low[:, 2 * HD : 3 * HD], high[:, 2 * HD : 3 * HD]], 1)
    mine = jnp.stack(by_distance(d_ffn))
    d_gate_up, d_down = assemble(mine, send(mine, "core", 1), jnp.stack([y, core]))
    return (
        result[None],
        grad_tokens[None],
        d_gains,
        d_head,
        d_split,
        d_shared,
        d_gate_up,
        d_down,
    )


def solution(mesh):
    fine = Mesh(mesh.devices.reshape(4, 2, 4, 2, 2), ("z", "xh", "y", "core", "tp"))
    fsdp, ctx, tp = ("z", "xh"), ("y", "core"), "tp"
    in_specs = (
        P(fsdp, ctx, None),
        P(fsdp, ctx),
        P(fsdp, None),
        P(),
        P(fsdp, None, tp),
        P(fsdp, None, None),
        P(fsdp, None, tp),
        P(fsdp, tp),
        P(fsdp, ctx, None),
    )
    out_specs = (
        P(fsdp, ctx, None),
        P(fsdp, ctx, None),
        P(fsdp, None),
        P(),
        P(fsdp, None, tp),
        P(fsdp, None, None),
        P(fsdp, None, tp),
        P(fsdp, tp),
    )
    return jax.shard_map(
        on_device, mesh=fine, in_specs=in_specs, out_specs=out_specs, check_vma=False
    )
```
